32 devices in a mesh: grp: 2 (over y), tm: 4 (over z), space: 4 (over x, core).
Axes of the slice: x: 2, y: 2, z: 4, core: 2. Of those that a mesh axis runs over, the one named last changes fastest.
Arguments:
- inputs: float32 [16, 8, 64, 128], P(('grp', 'tm'), 'space'), parts along dimension 0, may hold values from -6 to 6
- pre_first: float32 [16, 8, 64, 128], P(('grp', 'tm'), 'space'), parts along dimension 0, may hold values from -8 to 8
- pre_second: float32 [16, 8, 64, 128], P(('grp', 'tm'), 'space'), parts along dimension 0, may hold values from -8 to 8
- cotangent: float32 [16, 8, 64, 128], P(('grp', 'tm'), 'space'), parts along dimension 0, may hold values from -6 to 6
- weight_first: float32 [27, 128, 128], P(None, 'space'), may hold values from -0.109375 to 0.109375
- weight_second: float32 [27, 128, 128], P(None, 'space'), may hold values from -0.109375 to 0.109375
- clip_lengths: int32 [8], P('grp'), parts along dimension 0, may hold values from 1 to 4, as said below
Outputs:
- grad_inputs: float32 [16, 8, 64, 128], P(('grp', 'tm'), 'space'), parts along dimension 0
- grad_first: float32 [54, 128, 128], P('grp', 'space'), parts along dimension 0
- grad_second: float32 [54, 128, 128], P('grp', 'space'), parts along dimension 0
The draws below stay inside these ranges and needn't reach their ends.
There are 2 independent parts, one for each index of `grp`. The reference program is written for one: setup_inputs(seed, part) draws one part's arguments, and reference() takes and returns one part's arrays. A program takes and returns all parts, laid end to end along the dimension named above; an argument that names none is the same for every part. Nothing has to cross between parts.
Inputs may be any that keep to these rules, and one draw needn't show every extreme that they name: `clip_lengths`: the clip lengths sum to 8, and the longest is exactly 4.
All inputs are finite; a program needn't handle non-finite values.
Results may differ from the reference program's by a relative error of at most 0.0001.
Values sent between devices are 32-bit elements; how exact they have to be, the bound alone decides.
A program may use at most 64 MiB of HBM per device.

```python
import jax
import jax.numpy as jnp
from jax import lax

C = 128
WID = 64
NCLIP = 4
TFR = 8
HGT = 8


def draw_clip_lengths(key, part):
    longest = TFR // 2
    remain = TFR - longest
    key_cut = jax.random.fold_in(key, 11)
    key_pos = jax.random.fold_in(key, 23)
    order = jax.random.permutation(key_cut, jnp.arange(1, remain, dtype=jnp.int32))
    cuts = jnp.sort(order[:NCLIP - 2])
    edges = jnp.concatenate([jnp.zeros((1,), jnp.int32), cuts, jnp.full((1,), remain, jnp.int32)])
    others = edges[1:] - edges[:-1]
    place = jax.random.randint(key_pos, (), 0, NCLIP, dtype=jnp.int32)
    index = jnp.arange(NCLIP, dtype=jnp.int32)
    before = others[jnp.clip(index, 0, NCLIP - 2)]
    after = others[jnp.clip(index - 1, 0, NCLIP - 2)]
    result = jnp.where(index < place, before, jnp.where(index == place, longest, after))
    return result.astype(jnp.int32)


def block_scale(rng, extent, cuts, smallest, largest):
    factor_of = 1.0
    for position, shards_of in cuts:
        heights = jax.random.uniform(jax.random.fold_in(jax.random.fold_in(rng, 6), position), (shards_of,), jnp.float32, smallest / len(cuts), largest / len(cuts))
        factor_of = factor_of * jnp.repeat(jnp.exp(heights), extent[position] // shards_of).reshape((-1,) + (1,) * (len(extent) - 1 - position))
    return factor_of


def noise(rng, dims, deviation, limit, split=(), kind=jnp.bfloat16):
    array = jax.random.normal(rng, dims, jnp.float32) * deviation
    if len(split) > 0:
        array = block_scale(rng, dims, split, -0.22, 0.18) * array
    return jnp.clip(array, min=-limit, max=limit).astype(kind)


def setup_inputs(seed: int = 0, part: int = 0) -> dict:
    key_list = jax.random.split(jax.random.key(seed), 8)
    part_keys = jax.random.split(jax.random.fold_in(key_list[7], part), 8)
    return {
        "inputs": noise(part_keys[0], (TFR, HGT, WID, C), 1.0, 6.0, ((0, 4), (1, 4)), jnp.float32),
        "pre_first": noise(part_keys[1], (TFR, HGT, WID, C), 2.0, 8.0, ((0, 4), (1, 4)), jnp.float32),
        "pre_second": noise(part_keys[2], (TFR, HGT, WID, C), 2.0, 8.0, ((0, 4), (1, 4)), jnp.float32),
        "cotangent": noise(part_keys[3], (TFR, HGT, WID, C), 1.0, 6.0, ((0, 4), (1, 4)), jnp.float32),
        "weight_first": noise(key_list[4], (27, C, C), (27 * C) ** -0.5, 0.109375, ((1, 4),), jnp.float32),
        "weight_second": noise(key_list[5], (27, C, C), (27 * C) ** -0.5, 0.109375, ((1, 4),), jnp.float32),
        "clip_lengths": draw_clip_lengths(jax.random.fold_in(jax.random.fold_in(key_list[7], part), 71), part),
    }


def silu_slope(values):
    sigma = jax.nn.sigmoid(values)
    return sigma * (1.0 + values * (1.0 - sigma))

def clip_number(lengths, frames):
    endings = jnp.cumsum(lengths)
    return lax.optimization_barrier(jnp.sum((endings[None, :] <= frames[:, None]).astype(jnp.int32), axis=1))

def masked_views(grad, lengths):
    frames = grad.shape[0]
    padded = jnp.pad(grad, ((0, 2), (1, 1), (1, 1), (0, 0)))
    number = clip_number(lengths, jnp.arange(frames + 2, dtype=jnp.int32))
    views = []
    for ahead in range(3):
        same = (number[ahead:ahead + frames] == number[:frames]).astype(jnp.float32)
        views.append(padded[ahead:ahead + frames] * same[:, None, None, None])
    return views

def window_of(views, tap_t, tap_h, tap_w, height, breadth):
    chans = views[0].shape[3]
    part = views[2 - tap_t][:, 2 - tap_h:2 - tap_h + height, 2 - tap_w:2 - tap_w + breadth, :]
    return part.reshape(-1, chans)

def kernel_grad(fields, views):
    height, breadth, chans = (fields.shape[1], fields.shape[2], fields.shape[3])
    flat = fields.reshape(-1, chans)
    taps_out = []
    for tap_t in range(3):
        for tap_h in range(3):
            for tap_w in range(3):
                part = window_of(views, tap_t, tap_h, tap_w, height, breadth)
                taps_out.append(jnp.dot(flat.T, part, precision=lax.Precision.HIGHEST))
    return jnp.stack(taps_out)

def input_grad(views, weight, shape):
    height, breadth = (shape[1], shape[2])
    total = jnp.zeros((shape[0] * height * breadth, weight.shape[1]), jnp.float32)
    for tap_t in range(3):
        for tap_h in range(3):
            for tap_w in range(3):
                part = window_of(views, tap_t, tap_h, tap_w, height, breadth)
                total = total + jnp.dot(part, weight[9 * tap_t + 3 * tap_h + tap_w].T, precision=lax.Precision.HIGHEST)
    return total.reshape(shape[0], height, breadth, weight.shape[1])

def reference(inputs, pre_first, pre_second, cotangent, weight_first, weight_second, clip_lengths):
    factor = 1.0 / (inputs.shape[0] * inputs.shape[1] * inputs.shape[2]) ** 0.5
    grad_second_pre = cotangent * silu_slope(pre_second)
    views_second = masked_views(grad_second_pre, clip_lengths)
    grad_second = kernel_grad(jax.nn.silu(pre_first), views_second) * factor
    grad_hidden = input_grad(views_second, weight_second, inputs.shape)
    grad_first_pre = grad_hidden * silu_slope(pre_first)
    views_first = masked_views(grad_first_pre, clip_lengths)
    grad_first = kernel_grad(inputs, views_first) * factor
    grad_inputs = input_grad(views_first, weight_first, inputs.shape)
    return (grad_inputs, grad_first, grad_second)
```

```python
import functools
import itertools

import jax
import jax.numpy as jnp
from jax import lax
from jax.experimental import pallas as pl
from jax.experimental.pallas import tpu as pltpu
from jax.sharding import PartitionSpec as P

F32 = jnp.float32
BF16 = jnp.bfloat16


def silu_slope(values):
    sigma = 1.0 / (1.0 + jnp.exp(-values))
    return sigma * (1.0 + values * (1.0 - sigma))


def halves(values):
    high = values.astype(BF16)
    low = (values - high.astype(F32)).astype(BF16)
    return high, low


def kernel(
    dims,
    x_ref, p1_ref, p2_ref, ct_ref, w1_ref, w2_ref, len_ref,
    gi_ref, g1_ref, g2_ref,
    rows_buf, chan_buf, xp, xr, pp, pr, op, orr,
    gb2, gb1, wb2, wb1, ft2, ft1,
    part2, part1, rs2, rs1, full2, full1,
    send_sem, recv_sem,
):
    S, T, F, R, W, C, CI, NC, MP, B = dims
    X = S // 2
    H = S * R
    J = F * R
    tm = lax.axis_index("tm")
    s = lax.axis_index("space")
    core = lax.rem(s, 2)
    xi = s // 2
    sib = s + 1 - 2 * core
    count = itertools.count()
    sent = []

    def xpeer(d):
        return lax.rem(xi + d, X) * 2 + core

    def copy(src, dst, **target):
        i = next(count)
        c = pltpu.make_async_remote_copy(
            src_ref=src, dst_ref=dst, send_sem=send_sem.at[i], recv_sem=recv_sem.at[i],
            device_id=target, device_id_type=pl.DeviceIdType.MESH,
        )
        c.start()
        sent.append(c)
        return c

    def pack(pieces):
        tail = 128 - J * CI
        if tail:
            pieces = pieces + [jnp.zeros((W, tail), F32)]
        return jnp.concatenate(pieces, axis=1)

    barrier = pltpu.get_barrier_semaphore()
    for d in range(1, S):
        pl.semaphore_signal(barrier, inc=1, device_id={"space": lax.rem(s + d, S)}, device_id_type=pl.DeviceIdType.MESH)
    for d in range(1, T):
        pl.semaphore_signal(barrier, inc=1, device_id={"tm": lax.rem(tm + d, T)}, device_id_type=pl.DeviceIdType.MESH)

    ends = []
    run = jnp.int32(0)
    for j in range(NC):
        run = run + len_ref[j]
        ends.append(run)
    number = []
    for a in range(F + 2):
        frame = tm * F + a
        n = jnp.int32(0)
        for e in ends:
            n = n + jnp.where(e <= frame, jnp.int32(1), jnp.int32(0))
        number.append(n)
    mask = [[jnp.where(number[f + a] == number[f], F32(1.0), F32(0.0)) for a in range(3)] for f in range(F)]

    rows_buf[0, s] = ct_ref[...] * silu_slope(p2_ref[...])
    for b in range(S):
        pp[b] = pack([p1_ref[j * W:(j + 1) * W, b * CI:(b + 1) * CI] for j in range(J)])
    pl.semaphore_wait(barrier, S - 1 + T - 1)

    def spread(buf, half):
        near = copy(buf.at[half, s], buf.at[half, s], space=sib)
        far = [copy(buf.at[half, s], buf.at[half, s], space=xpeer(d)) for d in range(1, X)]
        return near, far

    def relay(buf, half, far):
        out = []
        for d in range(1, X):
            far[d - 1].wait_recv()
            origin = xpeer(X - d)
            out.append(copy(buf.at[half, origin], buf.at[half, origin], space=sib))
        return out

    def send_all(buf):
        back = copy(buf.at[0, s], buf.at[1, s], tm=lax.rem(tm + T - 1, T))
        near, far = spread(buf, 0)
        return back, near, far

    def exchange(src, dst):
        return [copy(src.at[lax.rem(s + d, S)], dst.at[s], space=lax.rem(s + d, S)) for d in range(1, S)]

    back, near, far = send_all(rows_buf)
    pcopies = exchange(pp, pr)
    pr[s] = pp[s]
    for b in range(S):
        xp[b] = pack([x_ref[j * W:(j + 1) * W, b * CI:(b + 1) * CI] for j in range(J)])
    xcopies = exchange(xp, xr)
    xr[s] = xp[s]

    def weights(w_ref, wb):
        wb[...] = jnp.zeros_like(wb)
        for kt in range(3):
            for kh in range(3):
                at = (3 * kt + kh) * 3 * CI
                high, low = halves(w_ref[at:at + 3 * CI, :])
                for dup in range(2):
                    c0 = kh * 2 * C + dup * C
                    wb[kt, 0:3 * CI, c0:c0 + C] = high
                    wb[kt, 128:128 + 3 * CI, c0:c0 + C] = low

    weights(w2_ref, wb2)
    for gb in (gb2, gb1):
        gb[:, 0] = jnp.zeros((2 * F, W, 2 * C), BF16)
        gb[:, H + 1] = jnp.zeros((2 * F, W, 2 * C), BF16)

    def finish(buf, back, near, far):
        out = relay(buf, 0, far)
        back.wait_recv()
        near1, far1 = spread(buf, 1)
        out += relay(buf, 1, far1)
        for c in [near, near1] + out:
            c.wait_recv()

    finish(rows_buf, back, near, far)
    for half in range(2):
        for b in range(S):
            for f in range(F):
                for r in range(R):
                    at = (f * R + r) * W
                    high, low = halves(rows_buf[half, b, at:at + W, :])
                    gb2[half * F + f, 1 + b * R + r, :, 0:C] = high
                    gb2[half * F + f, 1 + b * R + r, :, C:2 * C] = low

    pos = lax.rem(lax.broadcasted_iota(jnp.int32, (H * W, 128), 0), W)

    def input_grad(gb, wb):
        result = []
        for f in range(F):
            acc = None
            for kt in range(3):
                a = 2 - kt
                view = jnp.concatenate(
                    [gb[f + a, 2 - kh:2 - kh + H].reshape(H * W, 2 * C) for kh in range(3)], axis=1
                )
                d = lax.dot_general(view, wb[kt], (((1,), (1,)), ((), ())), preferred_element_type=F32)
                d = (d[:, 0:128] + d[:, 128:256]) * mask[f][a]
                acc = d if acc is None else acc + d
            up = jnp.where(pos == W - 1, 0.0, pltpu.roll(acc, H * W - 1, 0))
            down = jnp.where(pos == 0, 0.0, pltpu.roll(acc, 1, 0))
            result.append(up[:, 0:CI] + acc[:, CI:2 * CI] + down[:, 2 * CI:3 * CI])
        return result

    def packed_rows(parts, b):
        return pack([parts[f][(b * R + r) * W:(b * R + r + 1) * W, :] for f in range(F) for r in range(R)])

    hidden = input_grad(gb2, wb2)
    for c in pcopies:
        c.wait_recv()
    for b in range(S):
        chan_buf[0, s, b * W:(b + 1) * W, :] = packed_rows(hidden, b) * silu_slope(pr[b])
    back, near, far = send_all(chan_buf)

    wpos = lax.broadcasted_iota(jnp.int32, (W, 128), 0)

    def turned(fields, ft):
        cols = [[] for _ in range(F)]
        for b in range(S):
            mid = fields(b)
            down = jnp.where(wpos == 0, 0.0, pltpu.roll(mid, 1, 0))
            up = jnp.where(wpos == W - 1, 0.0, pltpu.roll(mid, W - 1, 0))
            for f in range(F):
                for r in range(R):
                    j = f * R + r
                    cols[f].append(jnp.concatenate(
                        [v[:, j * CI:(j + 1) * CI] for v in (down, mid, up)]
                        + [jnp.zeros((W, 128 - 3 * CI), F32)], axis=1))
        for f in range(F):
            whole = jnp.concatenate(cols[f], axis=0).T
            high, low = halves(whole[0:MP])
            ft[f, 0:MP] = high
            ft[f, MP:2 * MP] = low

    def kernel_grad(gb, ft, part):
        for kt in range(3):
            a = 2 - kt
            for kh in range(3):
                acc = None
                for f in range(F):
                    view = gb[f + a, 2 - kh:2 - kh + H].reshape(H * W, 2 * C)
                    d = jnp.dot(ft[f], view, preferred_element_type=F32)
                    d = (d[0:MP, 0:C] + d[MP:2 * MP, 0:C] + d[0:MP, C:2 * C]) * mask[f][a]
                    acc = d if acc is None else acc + d
                at = (3 * kt + kh) * 3 * CI
                part[at:at + 3 * CI, :] = acc[0:3 * CI]

    def silu(v):
        return v / (1.0 + jnp.exp(-v))

    def scatter(part, rs):
        out = []
        for d in range(1, T):
            to = lax.rem(tm + d, T)
            out.append(copy(part.at[pl.ds(pl.multiple_of(to * B, 8), B)], rs.at[tm], tm=to))
        return out

    scale = 1.0 / (F * T * H * W) ** 0.5

    def gather(copies, part, rs, full):
        for c in copies:
            c.wait_recv()
        mine = pl.ds(pl.multiple_of(tm * B, 8), B)
        total = part[mine, :]
        for d in range(1, T):
            total = total + rs[lax.rem(tm + d, T)]
        full[mine, :] = total * scale
        return [copy(full.at[mine], full.at[mine], tm=lax.rem(tm + d, T)) for d in range(1, T)]

    if T * B > 27 * CI:
        for part in (part2, part1):
            part[27 * CI:T * B, :] = jnp.zeros((T * B - 27 * CI, C), F32)

    turned(lambda b: silu(pr[b]), ft2)
    kernel_grad(gb2, ft2, part2)
    weights(w1_ref, wb1)
    finish(chan_buf, back, near, far)
    red2 = scatter(part2, rs2)
    for half in range(2):
        for b in range(S):
            for f in range(F):
                for r in range(R):
                    j = f * R + r
                    value = jnp.concatenate(
                        [chan_buf[half, q, b * W:(b + 1) * W, j * CI:(j + 1) * CI] for q in range(S)], axis=1)
                    high, low = halves(value)
                    gb1[half * F + f, 1 + b * R + r, :, 0:C] = high
                    gb1[half * F + f, 1 + b * R + r, :, C:2 * C] = low
    for c in xcopies:
        c.wait_recv()
    turned(lambda b: xr[b], ft1)
    kernel_grad(gb1, ft1, part1)
    red1 = scatter(part1, rs1)
    result = input_grad(gb1, wb1)
    for b in range(S):
        op[b] = packed_rows(result, b)
    ocopies = exchange(op, orr)
    orr[s] = op[s]
    all2 = gather(red2, part2, rs2, full2)
    all1 = gather(red1, part1, rs1, full1)
    for c in ocopies:
        c.wait_recv()
    for f in range(F):
        for r in range(R):
            j = f * R + r
            gi_ref[j * W:(j + 1) * W, :] = jnp.concatenate(
                [orr[q, :, j * CI:(j + 1) * CI] for q in range(S)], axis=1)
    for c in all2:
        c.wait_recv()
    g2_ref[...] = full2[0:27 * CI, :]
    for c in all1:
        c.wait_recv()
    g1_ref[...] = full1[0:27 * CI, :]
    for c in sent:
        c.wait_send()


def shards(S, T, inputs, pre_first, pre_second, cotangent, weight_first, weight_second, clip_lengths):
    F, R, W, C = inputs.shape
    CI = weight_first.shape[1]
    NC = clip_lengths.shape[0]
    X = S // 2
    H = S * R
    cells = F * R * W
    MP = -(-3 * CI // 16) * 16
    B = -(-27 * CI // (8 * T)) * 8
    n_sem = 2 * (1 + 2 * (1 + 2 * (X - 1))) + 3 * (S - 1) + 4 * (T - 1)
    dims = (S, T, F, R, W, C, CI, NC, MP, B)
    flat = lambda a: a.reshape(-1, a.shape[-1])
    vm = pl.BlockSpec(memory_space=pltpu.VMEM)
    piece = pltpu.VMEM((S, W, 128), F32)
    grad = pltpu.VMEM((T * B, C), F32)
    gi, g1, g2 = pl.pallas_call(
        functools.partial(kernel, dims),
        out_shape=(
            jax.ShapeDtypeStruct((cells, C), F32),
            jax.ShapeDtypeStruct((27 * CI, C), F32),
            jax.ShapeDtypeStruct((27 * CI, C), F32),
        ),
        in_specs=[vm] * 6 + [pl.BlockSpec(memory_space=pltpu.SMEM)],
        out_specs=(vm, vm, vm),
        scratch_shapes=[
            pltpu.VMEM((2, S, cells, C), F32),
            pltpu.VMEM((2, S, S * W, 128), F32),
            piece, piece, piece, piece, piece, piece,
            pltpu.VMEM((2 * F, H + 2, W, 2 * C), BF16),
            pltpu.VMEM((2 * F, H + 2, W, 2 * C), BF16),
            pltpu.VMEM((3, 256, 6 * C), BF16),
            pltpu.VMEM((3, 256, 6 * C), BF16),
            pltpu.VMEM((F, 2 * MP, H * W), BF16),
            pltpu.VMEM((F, 2 * MP, H * W), BF16),
            grad, grad,
            pltpu.VMEM((T, B, C), F32),
            pltpu.VMEM((T, B, C), F32),
            grad, grad,
            pltpu.SemaphoreType.DMA((n_sem,)),
            pltpu.SemaphoreType.DMA((n_sem,)),
        ],
        compiler_params=pltpu.CompilerParams(
            collective_id=0, has_side_effects=True, vmem_limit_bytes=56 * 1024 * 1024
        ),
    )(flat(inputs), flat(pre_first), flat(pre_second), flat(cotangent), flat(weight_first), flat(weight_second), clip_lengths)
    return gi.reshape(inputs.shape), g1.reshape(27, CI, C), g2.reshape(27, CI, C)


def solution(mesh):
    placed = (
        P(("grp", "tm"), "space", None, None),
        P(("grp", "tm"), "space", None, None),
        P(("grp", "tm"), "space", None, None),
        P(("grp", "tm"), "space", None, None),
        P(None, "space", None),
        P(None, "space", None),
        P("grp"),
    )
    return jax.shard_map(
        functools.partial(shards, mesh.shape["space"], mesh.shape["tm"]),
        mesh=mesh,
        in_specs=placed,
        out_specs=(
            P(("grp", "tm"), "space", None, None),
            P("grp", "space", None),
            P("grp", "space", None),
        ),
        check_vma=False,
    )
```

```python
import functools
import itertools

import jax
import jax.numpy as jnp
from jax import lax
from jax.experimental import pallas as pl
from jax.experimental.pallas import tpu as pltpu
from jax.sharding import PartitionSpec as P

F32 = jnp.float32
BF16 = jnp.bfloat16


def silu_slope(values):
    sigma = 1.0 / (1.0 + jnp.exp(-values))
    return sigma * (1.0 + values * (1.0 - sigma))


def halves(values):
    high = values.astype(BF16)
    low = (values - high.astype(F32)).astype(BF16)
    return high, low


def kernel(
    dims,
    x_ref, p1_ref, p2_ref, ct_ref, w1_ref, w2_ref, len_ref,
    gi_ref, g1_ref, g2_ref,
    rows_buf, chan_buf, xp, xr, pp, pr, op, orr,
    gb2, gb1, wb2, wb1, ft2, ft1,
    part2, part1, rs2, rs1, full2, full1,
    send_sem, recv_sem, line_send, line_recv,
):
    S, T, F, R, W, C, CI, NC, MP, B = dims
    X = S // 2
    H = S * R
    J = F * R
    tm = lax.axis_index("tm")
    s = lax.axis_index("space")
    core = lax.rem(s, 2)
    xi = s // 2
    sib = s + 1 - 2 * core
    count = itertools.count()
    sent = []

    def xpeer(d):
        return lax.rem(xi + d, X) * 2 + core

    def copy(src, dst, **target):
        i = next(count)
        c = pltpu.make_async_remote_copy(
            src_ref=src, dst_ref=dst, send_sem=send_sem.at[i], recv_sem=recv_sem.at[i],
            device_id=target, device_id_type=pl.DeviceIdType.MESH,
        )
        c.start()
        sent.append(c)
        return c

    def pack(pieces):
        tail = 128 - J * CI
        if tail:
            pieces = pieces + [jnp.zeros((W, tail), F32)]
        return jnp.concatenate(pieces, axis=1)

    barrier = pltpu.get_barrier_semaphore()
    for d in range(1, S):
        pl.semaphore_signal(barrier, inc=1, device_id={"space": lax.rem(s + d, S)}, device_id_type=pl.DeviceIdType.MESH)
    for d in range(1, T):
        pl.semaphore_signal(barrier, inc=1, device_id={"tm": lax.rem(tm + d, T)}, device_id_type=pl.DeviceIdType.MESH)

    ends = []
    run = jnp.int32(0)
    for j in range(NC):
        run = run + len_ref[j]
        ends.append(run)
    number = []
    for a in range(F + 2):
        frame = tm * F + a
        n = jnp.int32(0)
        for e in ends:
            n = n + jnp.where(e <= frame, jnp.int32(1), jnp.int32(0))
        number.append(n)
    mask = [[jnp.where(number[f + a] == number[f], F32(1.0), F32(0.0)) for a in range(3)] for f in range(F)]

    rows_buf[0, s] = ct_ref[...] * silu_slope(p2_ref[...])
    for b in range(S):
        pp[b] = pack([p1_ref[j * W:(j + 1) * W, b * CI:(b + 1) * CI] for j in range(J)])
    pl.semaphore_wait(barrier, S - 1 + T - 1)

    def spread(buf, half):
        near = copy(buf.at[half, s], buf.at[half, s], space=sib)
        far = [copy(buf.at[half, s], buf.at[half, s], space=xpeer(d)) for d in range(1, X)]
        return near, far

    def relay(buf, half, far):
        out = []
        for d in range(1, X):
            far[d - 1].wait_recv()
            origin = xpeer(X - d)
            out.append(copy(buf.at[half, origin], buf.at[half, origin], space=sib))
        return out

    after = lax.rem(tm + 1, T)
    before = lax.rem(tm + T - 1, T)

    def hop(g, stage, way, t, src, dst):
        return pltpu.make_async_remote_copy(
            src_ref=src, dst_ref=dst,
            send_sem=line_send.at[g, stage, way, t], recv_sem=line_recv.at[g, stage, way, t],
            device_id={"tm": before if way else after}, device_id_type=pl.DeviceIdType.MESH,
        )

    def halo(g, buf):
        return hop(g, 2, 1, 0, buf.at[0, s], buf.at[1, s])

    def send_all(g, buf):
        @pl.when(tm > 0)
        def _():
            halo(g, buf).start()

        @pl.when(tm == T - 1)
        def _():
            buf[1, s] = jnp.zeros(buf.shape[2:], F32)

        return spread(buf, 0)

    def exchange(src, dst):
        return [copy(src.at[lax.rem(s + d, S)], dst.at[s], space=lax.rem(s + d, S)) for d in range(1, S)]

    near, far = send_all(0, rows_buf)
    pr[s] = pp[s]
    for b in range(S):
        xp[b] = pack([x_ref[j * W:(j + 1) * W, b * CI:(b + 1) * CI] for j in range(J)])
    xr[s] = xp[s]

    def weights(w_ref, wb):
        wb[...] = jnp.zeros_like(wb)
        for kt in range(3):
            for kh in range(3):
                at = (3 * kt + kh) * 3 * CI
                high, low = halves(w_ref[at:at + 3 * CI, :])
                for dup in range(2):
                    c0 = kh * 2 * C + dup * C
                    wb[kt, 0:3 * CI, c0:c0 + C] = high
                    wb[kt, 128:128 + 3 * CI, c0:c0 + C] = low

    weights(w2_ref, wb2)
    for gb in (gb2, gb1):
        gb[:, 0] = jnp.zeros((2 * F, W, 2 * C), BF16)
        gb[:, H + 1] = jnp.zeros((2 * F, W, 2 * C), BF16)

    def finish(g, buf, near, far, between):
        @pl.when(tm < T - 1)
        def _():
            halo(g, buf).wait_recv()

        near1, far1 = spread(buf, 1)
        out = relay(buf, 0, far)
        more = between()
        out += relay(buf, 1, far1)
        for c in [near, near1] + out:
            c.wait_recv()
        return more

    pcopies = finish(0, rows_buf, near, far, lambda: exchange(pp, pr))
    xcopies = exchange(xp, xr)
    for half in range(2):
        for b in range(S):
            for f in range(F):
                for r in range(R):
                    at = (f * R + r) * W
                    high, low = halves(rows_buf[half, b, at:at + W, :])
                    gb2[half * F + f, 1 + b * R + r, :, 0:C] = high
                    gb2[half * F + f, 1 + b * R + r, :, C:2 * C] = low

    pos = lax.rem(lax.broadcasted_iota(jnp.int32, (H * W, 128), 0), W)

    def input_grad(gb, wb):
        result = []
        for f in range(F):
            acc = None
            for kt in range(3):
                a = 2 - kt
                view = jnp.concatenate(
                    [gb[f + a, 2 - kh:2 - kh + H].reshape(H * W, 2 * C) for kh in range(3)], axis=1
                )
                d = lax.dot_general(view, wb[kt], (((1,), (1,)), ((), ())), preferred_element_type=F32)
                d = (d[:, 0:128] + d[:, 128:256]) * mask[f][a]
                acc = d if acc is None else acc + d
            up = jnp.where(pos == W - 1, 0.0, pltpu.roll(acc, H * W - 1, 0))
            down = jnp.where(pos == 0, 0.0, pltpu.roll(acc, 1, 0))
            result.append(up[:, 0:CI] + acc[:, CI:2 * CI] + down[:, 2 * CI:3 * CI])
        return result

    def packed_rows(parts, b):
        return pack([parts[f][(b * R + r) * W:(b * R + r + 1) * W, :] for f in range(F) for r in range(R)])

    hidden = input_grad(gb2, wb2)
    for c in pcopies:
        c.wait_recv()
    for b in range(S):
        chan_buf[0, s, b * W:(b + 1) * W, :] = packed_rows(hidden, b) * silu_slope(pr[b])
    near, far = send_all(1, chan_buf)

    wpos = lax.broadcasted_iota(jnp.int32, (W, 128), 0)

    def turned(fields, ft):
        cols = [[] for _ in range(F)]
        for b in range(S):
            mid = fields(b)
            down = jnp.where(wpos == 0, 0.0, pltpu.roll(mid, 1, 0))
            up = jnp.where(wpos == W - 1, 0.0, pltpu.roll(mid, W - 1, 0))
            for f in range(F):
                for r in range(R):
                    j = f * R + r
                    cols[f].append(jnp.concatenate(
                        [v[:, j * CI:(j + 1) * CI] for v in (down, mid, up)]
                        + [jnp.zeros((W, 128 - 3 * CI), F32)], axis=1))
        for f in range(F):
            whole = jnp.concatenate(cols[f], axis=0).T
            high, low = halves(whole[0:MP])
            ft[f, 0:MP] = high
            ft[f, MP:2 * MP] = low

    def kernel_grad(gb, ft, part):
        for kt in range(3):
            a = 2 - kt
            for kh in range(3):
                acc = None
                for f in range(F):
                    view = gb[f + a, 2 - kh:2 - kh + H].reshape(H * W, 2 * C)
                    d = jnp.dot(ft[f], view, preferred_element_type=F32)
                    d = (d[0:MP, 0:C] + d[MP:2 * MP, 0:C] + d[0:MP, C:2 * C]) * mask[f][a]
                    acc = d if acc is None else acc + d
                at = (3 * kt + kh) * 3 * CI
                part[at:at + 3 * CI, :] = acc[0:3 * CI]

    def silu(v):
        return v / (1.0 + jnp.exp(-v))

    def block(ref, t):
        return ref.at[pl.ds(pl.multiple_of(t * B, 8), B)]

    def sum_hop(g, way, t, part, rs):
        return hop(g, 0, way, t, block(part, t), rs.at[way, t])

    def scatter_first(g, part, rs):
        @pl.when(tm == 0)
        def _():
            for t in range(T - 1, 0, -1):
                sum_hop(g, 0, t, part, rs).start()

        @pl.when(tm == T - 1)
        def _():
            for t in range(T - 1):
                sum_hop(g, 1, t, part, rs).start()

    def scatter_middle(g, part, rs):
        for k in range(T - 2):
            for way, t in ((0, T - 1 - k), (1, k)):
                inner = (tm > 0) & (tm < t) if way == 0 else (tm < T - 1) & (tm > t)

                @pl.when(inner)
                def _(way=way, t=t):
                    c = sum_hop(g, way, t, part, rs)
                    c.wait_recv()
                    part[t * B:(t + 1) * B, :] += rs[way, t]
                    c.start()

    scale = 1.0 / (F * T * H * W) ** 0.5

    def full_hop(g, way, t, full):
        return hop(g, 1, way, t, block(full, t), block(full, t))

    def own_block(g, part, rs, full):
        mine = pl.ds(pl.multiple_of(tm * B, 8), B)
        for way, has in ((0, tm > 0), (1, tm < T - 1)):
            @pl.when(has)
            def _(way=way):
                sum_hop(g, way, tm, part, rs).wait_recv()
                part[mine, :] += rs[way, tm]

        full[mine, :] = part[mine, :] * scale

        @pl.when(tm < T - 1)
        def _():
            full_hop(g, 0, tm, full).start()

        @pl.when(tm > 0)
        def _():
            full_hop(g, 1, tm, full).start()

    def pass_on(g, full):
        for k in range(1, T):
            @pl.when(tm - k >= 0)
            def _(k=k):
                c = full_hop(g, 0, tm - k, full)
                c.wait_recv()

                @pl.when(tm < T - 1)
                def _():
                    c.start()

            @pl.when(tm + k < T)
            def _(k=k):
                c = full_hop(g, 1, tm + k, full)
                c.wait_recv()

                @pl.when(tm > 0)
                def _():
                    c.start()

    def settle(g, buf, part, rs, full):
        @pl.when(tm > 0)
        def _():
            halo(g, buf).wait_send()

        for t in range(T):
            @pl.when((t > tm) & (tm < T - 1))
            def _(t=t):
                sum_hop(g, 0, t, part, rs).wait_send()

            @pl.when((t < tm) & (tm > 0))
            def _(t=t):
                sum_hop(g, 1, t, part, rs).wait_send()

            @pl.when((t <= tm) & (tm < T - 1))
            def _(t=t):
                full_hop(g, 0, t, full).wait_send()

            @pl.when((t >= tm) & (tm > 0))
            def _(t=t):
                full_hop(g, 1, t, full).wait_send()

    if T * B > 27 * CI:
        for part in (part2, part1):
            part[27 * CI:T * B, :] = jnp.zeros((T * B - 27 * CI, C), F32)

    turned(lambda b: silu(pr[b]), ft2)
    kernel_grad(gb2, ft2, part2)
    scatter_first(0, part2, rs2)
    weights(w1_ref, wb1)
    finish(1, chan_buf, near, far, lambda: scatter_middle(0, part2, rs2))
    for half in range(2):
        for b in range(S):
            for f in range(F):
                for r in range(R):
                    j = f * R + r
                    value = jnp.concatenate(
                        [chan_buf[half, q, b * W:(b + 1) * W, j * CI:(j + 1) * CI] for q in range(S)], axis=1)
                    high, low = halves(value)
                    gb1[half * F + f, 1 + b * R + r, :, 0:C] = high
                    gb1[half * F + f, 1 + b * R + r, :, C:2 * C] = low
    for c in xcopies:
        c.wait_recv()
    turned(lambda b: xr[b], ft1)
    kernel_grad(gb1, ft1, part1)
    scatter_first(1, part1, rs1)
    own_block(0, part2, rs2, full2)
    result = input_grad(gb1, wb1)
    for b in range(S):
        op[b] = packed_rows(result, b)
    ocopies = exchange(op, orr)
    orr[s] = op[s]
    scatter_middle(1, part1, rs1)
    pass_on(0, full2)
    own_block(1, part1, rs1, full1)
    g2_ref[...] = full2[0:27 * CI, :]
    for c in ocopies:
        c.wait_recv()
    for f in range(F):
        for r in range(R):
            j = f * R + r
            gi_ref[j * W:(j + 1) * W, :] = jnp.concatenate(
                [orr[q, :, j * CI:(j + 1) * CI] for q in range(S)], axis=1)
    pass_on(1, full1)
    g1_ref[...] = full1[0:27 * CI, :]
    settle(0, rows_buf, part2, rs2, full2)
    settle(1, chan_buf, part1, rs1, full1)
    for c in sent:
        c.wait_send()


def shards(S, T, inputs, pre_first, pre_second, cotangent, weight_first, weight_second, clip_lengths):
    F, R, W, C = inputs.shape
    CI = weight_first.shape[1]
    NC = clip_lengths.shape[0]
    X = S // 2
    H = S * R
    cells = F * R * W
    MP = -(-3 * CI // 16) * 16
    B = -(-27 * CI // (8 * T)) * 8
    n_sem = 4 * (1 + 2 * (X - 1)) + 3 * (S - 1)
    dims = (S, T, F, R, W, C, CI, NC, MP, B)
    flat = lambda a: a.reshape(-1, a.shape[-1])
    vm = pl.BlockSpec(memory_space=pltpu.VMEM)
    piece = pltpu.VMEM((S, W, 128), F32)
    grad = pltpu.VMEM((T * B, C), F32)
    gi, g1, g2 = pl.pallas_call(
        functools.partial(kernel, dims),
        out_shape=(
            jax.ShapeDtypeStruct((cells, C), F32),
            jax.ShapeDtypeStruct((27 * CI, C), F32),
            jax.ShapeDtypeStruct((27 * CI, C), F32),
        ),
        in_specs=[vm] * 6 + [pl.BlockSpec(memory_space=pltpu.SMEM)],
        out_specs=(vm, vm, vm),
        scratch_shapes=[
            pltpu.VMEM((2, S, cells, C), F32),
            pltpu.VMEM((2, S, S * W, 128), F32),
            piece, piece, piece, piece, piece, piece,
            pltpu.VMEM((2 * F, H + 2, W, 2 * C), BF16),
            pltpu.VMEM((2 * F, H + 2, W, 2 * C), BF16),
            pltpu.VMEM((3, 256, 6 * C), BF16),
            pltpu.VMEM((3, 256, 6 * C), BF16),
            pltpu.VMEM((F, 2 * MP, H * W), BF16),
            pltpu.VMEM((F, 2 * MP, H * W), BF16),
            grad, grad,
            pltpu.VMEM((2, T, B, C), F32),
            pltpu.VMEM((2, T, B, C), F32),
            grad, grad,
            pltpu.SemaphoreType.DMA((n_sem,)),
            pltpu.SemaphoreType.DMA((n_sem,)),
            pltpu.SemaphoreType.DMA((2, 3, 2, T)),
            pltpu.SemaphoreType.DMA((2, 3, 2, T)),
        ],
        compiler_params=pltpu.CompilerParams(
            collective_id=0, has_side_effects=True, vmem_limit_bytes=56 * 1024 * 1024
        ),
    )(flat(inputs), flat(pre_first), flat(pre_second), flat(cotangent), flat(weight_first), flat(weight_second), clip_lengths)
    return gi.reshape(inputs.shape), g1.reshape(27, CI, C), g2.reshape(27, CI, C)


def solution(mesh):
    placed = (
        P(("grp", "tm"), "space", None, None),
        P(("grp", "tm"), "space", None, None),
        P(("grp", "tm"), "space", None, None),
        P(("grp", "tm"), "space", None, None),
        P(None, "space", None),
        P(None, "space", None),
        P("grp"),
    )
    return jax.shard_map(
        functools.partial(shards, mesh.shape["space"], mesh.shape["tm"]),
        mesh=mesh,
        in_specs=placed,
        out_specs=(
            P(("grp", "tm"), "space", None, None),
            P("grp", "space", None),
            P("grp", "space", None),
        ),
        check_vma=False,
    )
```

```python
import functools
import itertools

import jax
import jax.numpy as jnp
from jax import lax
from jax.experimental import pallas as pl
from jax.experimental.pallas import tpu as pltpu
from jax.sharding import PartitionSpec as P

F32 = jnp.float32
BF16 = jnp.bfloat16


def silu_slope(values):
    sigma = 1.0 / (1.0 + jnp.exp(-values))
    return sigma * (1.0 + values * (1.0 - sigma))


def halves(values):
    high = values.astype(BF16)
    low = (values - high.astype(F32)).astype(BF16)
    return high, low


def kernel(
    dims,
    x_ref, p1_ref, p2_ref, ct_ref, w1_ref, w2_ref, len_ref,
    gi_ref, g1_ref, g2_ref,
    rows_buf, chan_buf, xp, xr, pp, pr, op, orr,
    gb2, gb1, wb2, wb1, ft2, ft1,
    part2, part1, rs2, rs1, full2, full1,
    send_sem, recv_sem, line_send, line_recv,
):
    S, T, F, R, W, C, CI, NC, MP, B = dims
    X = S // 2
    H = S * R
    J = F * R
    tm = lax.axis_index("tm")
    s = lax.axis_index("space")
    core = lax.rem(s, 2)
    xi = s // 2
    sib = s + 1 - 2 * core
    count = itertools.count()
    sent = []

    def xpeer(d):
        return lax.rem(xi + d, X) * 2 + core

    def copy(src, dst, **target):
        i = next(count)
        c = pltpu.make_async_remote_copy(
            src_ref=src, dst_ref=dst, send_sem=send_sem.at[i], recv_sem=recv_sem.at[i],
            device_id=target, device_id_type=pl.DeviceIdType.MESH,
        )
        c.start()
        sent.append(c)
        return c

    def pack(pieces):
        tail = 128 - J * CI
        if tail:
            pieces = pieces + [jnp.zeros((W, tail), F32)]
        return jnp.concatenate(pieces, axis=1)

    barrier = pltpu.get_barrier_semaphore()
    for d in range(1, S):
        pl.semaphore_signal(barrier, inc=1, device_id={"space": lax.rem(s + d, S)}, device_id_type=pl.DeviceIdType.MESH)
    for d in range(1, T):
        pl.semaphore_signal(barrier, inc=1, device_id={"tm": lax.rem(tm + d, T)}, device_id_type=pl.DeviceIdType.MESH)

    ends = []
    run = jnp.int32(0)
    for j in range(NC):
        run = run + len_ref[j]
        ends.append(run)
    number = []
    for a in range(F + 2):
        frame = tm * F + a
        n = jnp.int32(0)
        for e in ends:
            n = n + jnp.where(e <= frame, jnp.int32(1), jnp.int32(0))
        number.append(n)
    mask = [[jnp.where(number[f + a] == number[f], F32(1.0), F32(0.0)) for a in range(3)] for f in range(F)]

    rows_buf[0, s] = ct_ref[...] * silu_slope(p2_ref[...])
    for b in range(S):
        pp[b] = pack([p1_ref[j * W:(j + 1) * W, b * CI:(b + 1) * CI] for j in range(J)])
    pl.semaphore_wait(barrier, S - 1 + T - 1)

    def spread(buf, half):
        near = copy(buf.at[half, s], buf.at[half, s], space=sib)
        far = [copy(buf.at[half, s], buf.at[half, s], space=xpeer(d)) for d in range(1, X)]
        return near, far

    def relay(buf, half, far):
        out = []
        for d in range(1, X):
            far[d - 1].wait_recv()
            origin = xpeer(X - d)
            out.append(copy(buf.at[half, origin], buf.at[half, origin], space=sib))
        return out

    after = lax.rem(tm + 1, T)
    before = lax.rem(tm + T - 1, T)

    def hop(g, stage, way, t, src, dst):
        return pltpu.make_async_remote_copy(
            src_ref=src, dst_ref=dst,
            send_sem=line_send.at[g, stage, way, t], recv_sem=line_recv.at[g, stage, way, t],
            device_id={"tm": before if way else after}, device_id_type=pl.DeviceIdType.MESH,
        )

    def halo(g, buf):
        return hop(g, 2, 1, 0, buf.at[0, s], buf.at[1, s])

    def send_all(g, buf):
        @pl.when(tm > 0)
        def _():
            halo(g, buf).start()

        @pl.when(tm == T - 1)
        def _():
            buf[1, s] = jnp.zeros(buf.shape[2:], F32)

        return spread(buf, 0)

    def exchange(src, dst):
        return [copy(src.at[lax.rem(s + d, S)], dst.at[s], space=lax.rem(s + d, S)) for d in range(1, S)]

    near, far = send_all(0, rows_buf)
    pr[s] = pp[s]
    for b in range(S):
        xp[b] = pack([x_ref[j * W:(j + 1) * W, b * CI:(b + 1) * CI] for j in range(J)])
    xr[s] = xp[s]

    def weights(w_ref, wb):
        wb[...] = jnp.zeros_like(wb)
        for kt in range(3):
            for kh in range(3):
                at = (3 * kt + kh) * 3 * CI
                high, low = halves(w_ref[at:at + 3 * CI, :])
                for dup in range(2):
                    c0 = kh * 2 * C + dup * C
                    wb[kt, 0:3 * CI, c0:c0 + C] = high
                    wb[kt, 128:128 + 3 * CI, c0:c0 + C] = low

    weights(w2_ref, wb2)
    for gb in (gb2, gb1):
        gb[:, 0] = jnp.zeros((2 * F, W, 2 * C), BF16)
        gb[:, H + 1] = jnp.zeros((2 * F, W, 2 * C), BF16)

    def finish(g, buf, near, far, between):
        @pl.when(tm < T - 1)
        def _():
            halo(g, buf).wait_recv()

        near1, far1 = spread(buf, 1)
        out = relay(buf, 0, far)
        more = between()
        out += relay(buf, 1, far1)
        for c in [near, near1] + out:
            c.wait_recv()
        return more

    pcopies = finish(0, rows_buf, near, far, lambda: exchange(pp, pr))
    xcopies = exchange(xp, xr)
    for half in range(2):
        for b in range(S):
            for f in range(F):
                for r in range(R):
                    at = (f * R + r) * W
                    high, low = halves(rows_buf[half, b, at:at + W, :])
                    gb2[half * F + f, 1 + b * R + r, :, 0:C] = high
                    gb2[half * F + f, 1 + b * R + r, :, C:2 * C] = low

    pos = lax.rem(lax.broadcasted_iota(jnp.int32, (H * W, 128), 0), W)

    def input_grad(gb, wb):
        result = []
        for f in range(F):
            acc = None
            for kt in range(3):
                a = 2 - kt
                view = jnp.concatenate(
                    [gb[f + a, 2 - kh:2 - kh + H].reshape(H * W, 2 * C) for kh in range(3)], axis=1
                )
                d = lax.dot_general(view, wb[kt], (((1,), (1,)), ((), ())), preferred_element_type=F32)
                d = (d[:, 0:128] + d[:, 128:256]) * mask[f][a]
                acc = d if acc is None else acc + d
            up = jnp.where(pos == W - 1, 0.0, pltpu.roll(acc, H * W - 1, 0))
            down = jnp.where(pos == 0, 0.0, pltpu.roll(acc, 1, 0))
            result.append(up[:, 0:CI] + acc[:, CI:2 * CI] + down[:, 2 * CI:3 * CI])
        return result

    def packed_rows(parts, b):
        return pack([parts[f][(b * R + r) * W:(b * R + r + 1) * W, :] for f in range(F) for r in range(R)])

    hidden = input_grad(gb2, wb2)
    for c in pcopies:
        c.wait_recv()
    for b in range(S):
        chan_buf[0, s, b * W:(b + 1) * W, :] = packed_rows(hidden, b) * silu_slope(pr[b])
    near, far = send_all(1, chan_buf)

    wpos = lax.broadcasted_iota(jnp.int32, (W, 128), 0)

    def turned(fields, ft):
        cols = [[] for _ in range(F)]
        for b in range(S):
            mid = fields(b)
            down = jnp.where(wpos == 0, 0.0, pltpu.roll(mid, 1, 0))
            up = jnp.where(wpos == W - 1, 0.0, pltpu.roll(mid, W - 1, 0))
            for f in range(F):
                for r in range(R):
                    j = f * R + r
                    cols[f].append(jnp.concatenate(
                        [v[:, j * CI:(j + 1) * CI] for v in (down, mid, up)]
                        + [jnp.zeros((W, 128 - 3 * CI), F32)], axis=1))
        for f in range(F):
            whole = jnp.concatenate(cols[f], axis=0).T
            high, low = halves(whole[0:MP])
            ft[f, 0:MP] = high
            ft[f, MP:2 * MP] = low

    def kernel_grad(gb, ft, part):
        for kt in range(3):
            a = 2 - kt
            for kh in range(3):
                acc = None
                for f in range(F):
                    view = gb[f + a, 2 - kh:2 - kh + H].reshape(H * W, 2 * C)
                    d = jnp.dot(ft[f], view, preferred_element_type=F32)
                    d = (d[0:MP, 0:C] + d[MP:2 * MP, 0:C] + d[0:MP, C:2 * C]) * mask[f][a]
                    acc = d if acc is None else acc + d
                at = (3 * kt + kh) * 3 * CI
                part[at:at + 3 * CI, :] = acc[0:3 * CI]

    def silu(v):
        return v / (1.0 + jnp.exp(-v))

    def block(ref, t):
        return ref.at[pl.ds(pl.multiple_of(t * B, 8), B)]

    def sum_hop(g, way, t, part, rs):
        return hop(g, 0, way, t, block(part, t), rs.at[way, t])

    def scatter_first(g, part, rs):
        @pl.when(tm == 0)
        def _():
            for t in range(T - 1, 0, -1):
                sum_hop(g, 0, t, part, rs).start()

        @pl.when(tm == T - 1)
        def _():
            for t in range(T - 1):
                sum_hop(g, 1, t, part, rs).start()

    def scatter_middle(g, part, rs):
        def right():
            for t in range(T - 1, 1, -1):
                @pl.when(tm < t)
                def _(t=t):
                    c = sum_hop(g, 0, t, part, rs)
                    c.wait_recv()
                    part[t * B:(t + 1) * B, :] += rs[0, t]
                    c.start()

        def left():
            for t in range(T - 2):
                @pl.when(tm > t)
                def _(t=t):
                    c = sum_hop(g, 1, t, part, rs)
                    c.wait_recv()
                    part[t * B:(t + 1) * B, :] += rs[1, t]
                    c.start()

        @pl.when((tm > 0) & (tm < T // 2))
        def _():
            right()
            left()

        @pl.when((tm < T - 1) & (tm >= T // 2))
        def _():
            left()
            right()

    scale = 1.0 / (F * T * H * W) ** 0.5

    def full_hop(g, way, t, full):
        return hop(g, 1, way, t, block(full, t), block(full, t))

    def own_block(g, part, rs, full):
        mine = pl.ds(pl.multiple_of(tm * B, 8), B)
        for way, has in ((0, tm > 0), (1, tm < T - 1)):
            @pl.when(has)
            def _(way=way):
                sum_hop(g, way, tm, part, rs).wait_recv()
                part[mine, :] += rs[way, tm]

        full[mine, :] = part[mine, :] * scale

        @pl.when(tm < T - 1)
        def _():
            full_hop(g, 0, tm, full).start()

        @pl.when(tm > 0)
        def _():
            full_hop(g, 1, tm, full).start()

    def pass_on(g, full, steps):
        for k in steps:
            @pl.when(tm - k >= 0)
            def _(k=k):
                c = full_hop(g, 0, tm - k, full)
                c.wait_recv()

                @pl.when(tm < T - 1)
                def _():
                    c.start()

            @pl.when(tm + k < T)
            def _(k=k):
                c = full_hop(g, 1, tm + k, full)
                c.wait_recv()

                @pl.when(tm > 0)
                def _():
                    c.start()

    def settle(g, buf, part, rs, full):
        @pl.when(tm > 0)
        def _():
            halo(g, buf).wait_send()

        for t in range(T):
            @pl.when((t > tm) & (tm < T - 1))
            def _(t=t):
                sum_hop(g, 0, t, part, rs).wait_send()

            @pl.when((t < tm) & (tm > 0))
            def _(t=t):
                sum_hop(g, 1, t, part, rs).wait_send()

            @pl.when((t <= tm) & (tm < T - 1))
            def _(t=t):
                full_hop(g, 0, t, full).wait_send()

            @pl.when((t >= tm) & (tm > 0))
            def _(t=t):
                full_hop(g, 1, t, full).wait_send()

    if T * B > 27 * CI:
        for part in (part2, part1):
            part[27 * CI:T * B, :] = jnp.zeros((T * B - 27 * CI, C), F32)

    turned(lambda b: silu(pr[b]), ft2)
    kernel_grad(gb2, ft2, part2)
    scatter_first(0, part2, rs2)
    weights(w1_ref, wb1)
    finish(1, chan_buf, near, far, lambda: None)
    scatter_middle(0, part2, rs2)
    for half in range(2):
        for b in range(S):
            for f in range(F):
                for r in range(R):
                    j = f * R + r
                    value = jnp.concatenate(
                        [chan_buf[half, q, b * W:(b + 1) * W, j * CI:(j + 1) * CI] for q in range(S)], axis=1)
                    high, low = halves(value)
                    gb1[half * F + f, 1 + b * R + r, :, 0:C] = high
                    gb1[half * F + f, 1 + b * R + r, :, C:2 * C] = low
    for c in xcopies:
        c.wait_recv()
    turned(lambda b: xr[b], ft1)
    own_block(0, part2, rs2, full2)
    kernel_grad(gb1, ft1, part1)
    scatter_first(1, part1, rs1)
    pass_on(0, full2, range(1, 2))
    result = input_grad(gb1, wb1)
    for b in range(S):
        op[b] = packed_rows(result, b)
    ocopies = exchange(op, orr)
    orr[s] = op[s]
    scatter_middle(1, part1, rs1)
    pass_on(0, full2, range(2, T))
    own_block(1, part1, rs1, full1)
    g2_ref[...] = full2[0:27 * CI, :]
    for c in ocopies:
        c.wait_recv()
    for f in range(F):
        for r in range(R):
            j = f * R + r
            gi_ref[j * W:(j + 1) * W, :] = jnp.concatenate(
                [orr[q, :, j * CI:(j + 1) * CI] for q in range(S)], axis=1)
    pass_on(1, full1, range(1, T))
    g1_ref[...] = full1[0:27 * CI, :]
    settle(0, rows_buf, part2, rs2, full2)
    settle(1, chan_buf, part1, rs1, full1)
    for c in sent:
        c.wait_send()


def hand_over(a, b, c, x, y, z):
    x[...] = a[...]
    y[...] = b[...]
    z[...] = c[...]


def shards(S, T, inputs, pre_first, pre_second, cotangent, weight_first, weight_second, clip_lengths):
    F, R, W, C = inputs.shape
    CI = weight_first.shape[1]
    NC = clip_lengths.shape[0]
    X = S // 2
    H = S * R
    cells = F * R * W
    MP = -(-3 * CI // 16) * 16
    B = -(-27 * CI // (8 * T)) * 8
    n_sem = 4 * (1 + 2 * (X - 1)) + 3 * (S - 1)
    dims = (S, T, F, R, W, C, CI, NC, MP, B)
    flat = lambda a: a.reshape(-1, a.shape[-1])
    vm = pl.BlockSpec(memory_space=pltpu.VMEM)
    piece = pltpu.VMEM((S, W, 128), F32)
    grad = pltpu.VMEM((T * B, C), F32)
    gi, g1, g2 = pl.pallas_call(
        functools.partial(kernel, dims),
        out_shape=(
            jax.ShapeDtypeStruct((cells, C), F32),
            jax.ShapeDtypeStruct((27 * CI, C), F32),
            jax.ShapeDtypeStruct((27 * CI, C), F32),
        ),
        in_specs=[vm] * 6 + [pl.BlockSpec(memory_space=pltpu.SMEM)],
        out_specs=(vm, vm, vm),
        scratch_shapes=[
            pltpu.VMEM((2, S, cells, C), F32),
            pltpu.VMEM((2, S, S * W, 128), F32),
            piece, piece, piece, piece, piece, piece,
            pltpu.VMEM((2 * F, H + 2, W, 2 * C), BF16),
            pltpu.VMEM((2 * F, H + 2, W, 2 * C), BF16),
            pltpu.VMEM((3, 256, 6 * C), BF16),
            pltpu.VMEM((3, 256, 6 * C), BF16),
            pltpu.VMEM((F, 2 * MP, H * W), BF16),
            pltpu.VMEM((F, 2 * MP, H * W), BF16),
            grad, grad,
            pltpu.VMEM((2, T, B, C), F32),
            pltpu.VMEM((2, T, B, C), F32),
            grad, grad,
            pltpu.SemaphoreType.DMA((n_sem,)),
            pltpu.SemaphoreType.DMA((n_sem,)),
            pltpu.SemaphoreType.DMA((2, 3, 2, T)),
            pltpu.SemaphoreType.DMA((2, 3, 2, T)),
        ],
        compiler_params=pltpu.CompilerParams(
            collective_id=0, has_side_effects=True, vmem_limit_bytes=56 * 1024 * 1024
        ),
    )(flat(inputs), flat(pre_first), flat(pre_second), flat(cotangent), flat(weight_first), flat(weight_second), clip_lengths)
    anywhere = pl.BlockSpec(memory_space=pltpu.VMEM)
    gi, g1, g2 = pl.pallas_call(
        hand_over,
        out_shape=tuple(jax.ShapeDtypeStruct(v.shape, F32) for v in (gi, g1, g2)),
        in_specs=[anywhere] * 3,
        out_specs=(anywhere,) * 3,
    )(gi, g1, g2)
    return gi.reshape(inputs.shape), g1.reshape(27, CI, C), g2.reshape(27, CI, C)


def solution(mesh):
    placed = (
        P(("grp", "tm"), "space", None, None),
        P(("grp", "tm"), "space", None, None),
        P(("grp", "tm"), "space", None, None),
        P(("grp", "tm"), "space", None, None),
        P(None, "space", None),
        P(None, "space", None),
        P("grp"),
    )
    return jax.shard_map(
        functools.partial(shards, mesh.shape["space"], mesh.shape["tm"]),
        mesh=mesh,
        in_specs=placed,
        out_specs=(
            P(("grp", "tm"), "space", None, None),
            P("grp", "space", None),
            P("grp", "space", None),
        ),
        check_vma=False,
    )
```
